32 devices in a mesh: grp: 2 (over y), row: 4 (over z), col: 2 (over x), rep: 2 (over core).
Axes of the slice: x: 2, y: 2, z: 4, core: 2. Of those that a mesh axis runs over, the one named last changes fastest.
Arguments:
- shard_rows: bfloat16 [11520, 512], P(('grp', 'row', 'col', 'rep')), parts along dimension 0, may hold values from -24 to 24
- row_position: int32 [11520], P(('grp', 'row', 'col', 'rep')), parts along dimension 0, may hold values from 0 to 3071, as said below
- shard_count: int32 [32], P(('grp', 'row', 'col', 'rep')), parts along dimension 0, may hold values from 1 to 360, as said below
Outputs:
- max_similarity: float32 [6144], P(('grp', 'row', 'col', 'rep')), parts along dimension 0
The draws below stay inside these ranges and needn't reach their ends.
There are 2 independent parts, one for each index of `grp`. The reference program is written for one: setup_inputs(seed, part) draws one part's arguments, and reference() takes and returns one part's arrays. A program takes and returns all parts, laid end to end along the dimension named above; each array names one. Nothing has to cross between parts.
Inputs may be any that keep to these rules, and one draw needn't show every extreme that they name: `row_position`: row j of shard s is used when j < shard_count[s]; the used rows of all shards hold every position 0 to 3071 once, unused rows hold arbitrary positions. At most 24 used rows of one shard have positions in one aligned run of 192 positions, and some shard reaches 24. `shard_count`: the counts sum to 3072.
All inputs are finite; a program needn't handle non-finite values.
Results may differ from the reference program's by a relative error of at most 0.00063.
Values may be sent and summed in bfloat16 or wider, within the bound.
A program may use at most 64 MiB of HBM per device.

```python
import math
import jax
import jax.numpy as jnp
from jax import lax

D = 512
OWN = 192
SHARDS = 16
MEMBERS = 3072
LOAD = 12
EXTRA = 168
CAP = 360


def layout(key):
    base_key = jax.random.fold_in(key, 7)
    streams = jax.random.split(base_key, 5)
    shards_at = jnp.arange(SHARDS, dtype=jnp.int32)
    heavy = (jax.random.permutation(streams[0], SHARDS) < SHARDS // 8).astype(jnp.int32) * LOAD
    ranked = jax.random.permutation(streams[1], SHARDS)
    full_runs = EXTRA // LOAD
    spread = jnp.where(ranked < full_runs, LOAD, jnp.where(ranked == full_runs, EXTRA % LOAD, 0)).astype(jnp.int32)
    offsets = (shards_at[:, None] - shards_at[None, :]) % SHARDS
    loads = heavy[:, None] + spread[offsets]
    counts = jnp.sum(loads, 1)
    ending = jnp.cumsum(loads, 1)
    earlier = jnp.cumsum(loads, 0) - loads
    slot_index = jnp.arange(CAP, dtype=jnp.int32)
    owner = jax.vmap(lambda bounds: jnp.searchsorted(bounds, slot_index, side='right'))(ending)
    owner = jnp.minimum(owner, SHARDS - 1).astype(jnp.int32)
    begins = jnp.take_along_axis(ending - loads, owner, 1)
    within = jnp.take_along_axis(earlier, owner, 1) + slot_index[None, :] - begins
    within = jnp.clip(within, 0, OWN - 1)
    orders = jax.vmap(lambda number: jax.random.permutation(jax.random.fold_in(streams[2], number), OWN))(shards_at)
    picked = orders[owner, within]
    is_used = slot_index[None, :] < counts[:, None]
    filler = jax.random.randint(streams[3], (SHARDS, CAP), 0, MEMBERS)
    position = jnp.where(is_used, owner * OWN + picked, filler)
    noise = jax.random.randint(streams[4], (SHARDS, CAP), 0, 2 ** 19)
    scores = jnp.where(is_used, noise * CAP + slot_index[None, :], 2 ** 30 + slot_index[None, :])
    shuffle = jnp.argsort(scores, axis=1, stable=True)
    position = jnp.take_along_axis(position, shuffle, 1)
    return (position.astype(jnp.int32), counts.astype(jnp.int32), is_used)


def draw_row_position(key, part):
    return layout(key)[0].reshape(SHARDS * CAP)


def draw_shard_count(key, part):
    return layout(key)[1]


def draw_shard_rows(key, part):
    position, counts, is_used = layout(key)
    streams = jax.random.split(jax.random.fold_in(key, 11), 6)
    pairing = jax.random.permutation(streams[0], MEMBERS)
    partner = jnp.zeros((MEMBERS,), jnp.int32).at[pairing].set(jnp.arange(MEMBERS, dtype=jnp.int32) // 2)
    shared = jax.random.normal(streams[1], (MEMBERS // 2, D))
    strength = jax.random.uniform(streams[3], (MEMBERS // 2,), minval=0.0, maxval=0.97)[partner][:, None]
    private = jax.random.normal(streams[2], (MEMBERS, D))
    scaling = jnp.exp(jax.random.uniform(streams[4], (MEMBERS, 1), minval=-0.693, maxval=0.693))
    member = jnp.clip(strength * shared[partner] + jnp.sqrt(1.0 - strength * strength) * private, -6.0, 6.0) * scaling
    filler = jnp.clip(jax.random.normal(streams[5], (SHARDS, CAP, D)), -6.0, 6.0)
    result = jnp.where(is_used[:, :, None], member[position], filler)
    return result.reshape(SHARDS * CAP, D).astype(jnp.bfloat16)


def setup_inputs(seed: int = 0, part: int = 0) -> dict:
    key_of = jax.random.split(jax.random.key(seed), 4)
    part_splits = jax.random.split(jax.random.fold_in(key_of[3], part), 4)
    return {
        "shard_rows": draw_shard_rows(jax.random.fold_in(jax.random.fold_in(key_of[3], part), 71), part),
        "row_position": draw_row_position(jax.random.fold_in(jax.random.fold_in(key_of[3], part), 71), part),
        "shard_count": draw_shard_count(jax.random.fold_in(jax.random.fold_in(key_of[3], part), 71), part),
    }


def reference(shard_rows, row_position, shard_count):
    is_used = (jnp.arange(CAP, dtype=jnp.int32)[None, :] < shard_count[:, None]).reshape(-1)
    target = jnp.where(is_used, row_position, MEMBERS).astype(jnp.int32)
    members = jnp.zeros((MEMBERS, D), jnp.bfloat16).at[target].set(shard_rows, mode='drop')
    widened = members.astype(jnp.float32)
    normed = (widened / jnp.sqrt(lax.optimization_barrier(jnp.sum(widened * widened, 1, keepdims=True)) + 1e-06)).astype(jnp.bfloat16)
    row_step = math.gcd(MEMBERS, 256)
    every_column = jnp.arange(MEMBERS, dtype=jnp.int32)

    def row_maxima(row_start):
        row_tile = lax.dynamic_slice_in_dim(normed, row_start, row_step, 0)
        scores = jnp.dot(row_tile, normed.T, preferred_element_type=jnp.float32)
        row_global = row_start + jnp.arange(row_step, dtype=jnp.int32)
        scores = jnp.where(row_global[:, None] == every_column[None, :], -4.0, scores)
        return lax.optimization_barrier(jnp.max(scores, 1))
    starts = jnp.arange(MEMBERS // row_step, dtype=jnp.int32) * row_step
    return lax.map(row_maxima, starts).reshape(MEMBERS)
```

```python
import functools
import math

import jax
import jax.numpy as jnp
from jax import lax
from jax.experimental import pallas as pl
from jax.experimental.pallas import tpu as pltpu
from jax.sharding import PartitionSpec as P

OWN = 192


def normalize(owned_rows):
    widened = owned_rows.astype(jnp.float32)
    return (widened / jnp.sqrt(jnp.sum(widened * widened, 1, keepdims=True) + 1e-06)).astype(
        jnp.bfloat16
    )


def body(shard_rows, row_position, shard_count):
    row_devices = lax.axis_size("row")
    cross_devices = lax.axis_size(("col", "rep"))
    all_shards = row_devices * cross_devices
    per_owner = OWN
    owner_load = max(1, per_owner // all_shards)
    slot_count = 2 * owner_load
    block_rows = per_owner * cross_devices
    capacity, feature = shard_rows.shape
    row_place = lax.axis_index("row")
    cross_place = lax.axis_index(("col", "rep"))
    is_used = jnp.arange(capacity) < shard_count[0]
    position = jnp.where(is_used, row_position, 0)
    owner_first = position // per_owner
    one_hot = jnp.logical_and(
        owner_first[:, None] == jnp.arange(all_shards)[None, :], is_used[:, None]
    ).astype(jnp.int32)
    ranking = jnp.sum(jnp.cumsum(one_hot, 0) * one_hot, 1) - 1
    target = jnp.where(is_used, owner_first * slot_count + ranking, all_shards * slot_count)
    packed = (
        jnp.zeros((all_shards * slot_count, feature), shard_rows.dtype)
        .at[target]
        .set(shard_rows, mode="drop")
    )
    placed = (
        jnp.full((all_shards * slot_count,), -1, jnp.int32).at[target].set(position, mode="drop")
    )
    first_packed = packed.reshape(row_devices, cross_devices, slot_count, feature)
    first_placed = placed.reshape(row_devices, cross_devices, slot_count)
    own_offset = row_place * block_rows + cross_place * per_owner
    received = (
        lax.all_to_all(
            lax.all_to_all(first_packed, "row", split_axis=0, concat_axis=0, tiled=True),
            ("col", "rep"),
            split_axis=1,
            concat_axis=1,
            tiled=True,
        ),
        lax.all_to_all(
            lax.all_to_all(first_placed, "row", split_axis=0, concat_axis=0, tiled=True),
            ("col", "rep"),
            split_axis=1,
            concat_axis=1,
            tiled=True,
        ),
    )
    flat_rows = received[0].reshape(-1, feature)
    flat_places = received[1].reshape(-1)
    local_index = jnp.where(flat_places >= 0, flat_places - own_offset, per_owner)
    owned_rows = (
        jnp.zeros((per_owner, feature), flat_rows.dtype).at[local_index].set(flat_rows, mode="drop")
    )
    row_owned = normalize(owned_rows)
    row_block = lax.all_gather(row_owned, ("col", "rep"), axis=0, tiled=True)
    column_index = jnp.arange(block_rows)
    column_block = lax.all_gather(row_owned, "row", axis=0, tiled=True)
    column_places = (
        column_index // per_owner * block_rows + cross_place * per_owner + column_index % per_owner
    )
    row_step = math.gcd(block_rows, 512)
    column_step = math.gcd(block_rows, 1024)

    def row_maxima(inputs):
        row_tile, row_start = inputs
        row_global = row_place * block_rows + row_start + jnp.arange(row_step)
        running = jnp.full((row_step,), -4.0, jnp.float32)
        for column_turn in range(block_rows // column_step):
            column_tile = column_block[column_turn * column_step : (column_turn + 1) * column_step]
            scores = jnp.einsum(
                "rd,cd->rc", row_tile, column_tile, preferred_element_type=jnp.float32
            )
            column_global = column_places[
                column_turn * column_step : (column_turn + 1) * column_step
            ]
            scores = jnp.where(row_global[:, None] == column_global[None, :], -4.0, scores)
            running = jnp.maximum(running, jnp.max(scores, 1))
        return running

    starts = jnp.arange(block_rows // row_step, dtype=jnp.int32) * row_step
    maxima = lax.map(row_maxima, (row_block.reshape(-1, row_step, feature), starts)).reshape(
        block_rows
    )
    combined = lax.pmax(maxima, ("col", "rep"))
    return lax.dynamic_slice_in_dim(combined, cross_place * per_owner, per_owner)


FLOOR = -8.0
LANES = 128
SLOTS = 10


def line_kernel(
    capacity, sent, padded, chunks,
    rows_ref, place_ref, out_ref,
    buf, places, row_acc, col_acc, row_bias, col_bias, result, gathered, final_acc,
    send_sem, recv_sem, place_send, place_recv, final_send, final_recv,
):
    z, x, c = lax.axis_index("row"), lax.axis_index("col"), lax.axis_index("rep")
    me = z * 4 + x * 2 + c
    inner = jnp.logical_and(z >= 1, z <= 2)
    low = z <= 1
    leads = c == z - 1
    rank = (z - 1) * 4 + x * 2 + c

    def where_is(device):
        return {"row": device // 4, "col": (device // 2) % 2, "rep": device % 2}

    def at(zz, xx, cc):
        return {"row": zz, "col": xx, "rep": cc}

    def line_z(turn):
        ahead = (1, 0, 2, 3)[turn]
        return jnp.where(low, ahead, 3 - ahead)

    barrier = pltpu.get_barrier_semaphore()
    for step in range(1, 16):
        pl.semaphore_signal(
            barrier, inc=1, device_id=where_is((me + step) % 16), device_id_type=pl.DeviceIdType.MESH
        )

    widened = rows_ref[...].astype(jnp.float32)
    scale = jnp.sqrt(jnp.sum(widened * widened, 1, keepdims=True) + 1e-06)
    buf[0, :capacity] = (widened / scale).astype(jnp.bfloat16)
    if padded > capacity:
        buf[0, capacity:] = jnp.zeros((padded - capacity, buf.shape[2]), jnp.bfloat16)
    places[me] = place_ref[...]

    @pl.when(inner)
    def _():
        if padded > sent:
            for slot in range(1, SLOTS):
                buf[slot, sent:] = jnp.zeros((padded - sent, buf.shape[2]), jnp.bfloat16)
        row_acc[...] = jnp.full(row_acc.shape, FLOOR, jnp.float32)
        col_acc[...] = jnp.full(col_acc.shape, FLOOR, jnp.float32)
        result[...] = jnp.full(result.shape, FLOOR, jnp.float32)

    pl.semaphore_wait(barrier, 15)

    def copy(src, dst, kind, k, device):
        begin, count = chunks[k]
        return pltpu.make_async_remote_copy(
            src_ref=buf.at[src, pl.ds(begin, count)],
            dst_ref=buf.at[dst, pl.ds(begin, count)],
            send_sem=send_sem.at[kind, k],
            recv_sem=recv_sem.at[dst, k],
            device_id=device,
            device_id_type=pl.DeviceIdType.MESH,
        )

    every = range(len(chunks))
    inward = at(jnp.where(low, 1, 2), x, c)
    peer = at(3 - z, x, c)
    sister = at(z, x, 1 - c)
    across = at(z, 1, c)

    def arrived(slot, k):
        copy(slot, slot, 0, k, sister).wait_recv()

    @pl.when(jnp.logical_not(inner))
    def _():
        for k in every:
            copy(0, 1, 0, k, inward).start()

    @pl.when(inner)
    def _():
        for k in every:
            copy(0, 2, 0, k, peer).start()

        @pl.when(jnp.logical_and(leads, x == 0))
        def _():
            for k in every:
                copy(0, 6, 4, k, across).start()

        for k in every:
            copy(0, 4, 2, k, sister).start()

    def place_copy(step, origin, target):
        return pltpu.make_async_remote_copy(
            src_ref=place_ref,
            dst_ref=places.at[origin],
            send_sem=place_send.at[step],
            recv_sem=place_recv.at[step],
            device_id=where_is(target),
            device_id_type=pl.DeviceIdType.MESH,
        )

    for step in range(1, 16):
        place_copy(step, me, (me + step) % 16).start()
    for step in range(1, 16):
        place_copy(step, (me + 16 - step) % 16, (me + step) % 16).wait_recv()

    def pair(a, b, same=False):
        scores = lax.dot_general(
            buf[a], buf[b], (((1,), (1,)), ((), ())), preferred_element_type=jnp.float32
        )
        if same:
            row_id = lax.broadcasted_iota(jnp.int32, scores.shape, 0)
            col_id = lax.broadcasted_iota(jnp.int32, scores.shape, 1)
            scores = jnp.where(row_id == col_id, FLOOR, scores)
        bias = row_bias[a]
        running = None if same else row_acc[a]
        for j in range(padded // LANES):
            lanes = slice(j * LANES, (j + 1) * LANES)
            part = scores[:, lanes]
            down = jnp.max((part + bias).reshape(padded // 8, 8, LANES), 0)
            col_acc[b, :, lanes] = jnp.maximum(col_acc[b, :, lanes], down)
            if not same:
                running = jnp.maximum(running, part + col_bias[b][:, lanes])
        if not same:
            row_acc[a] = running

    def each(begin, end, fn):
        def step(i, carry):
            fn(i)
            return carry

        lax.fori_loop(begin, end, step, 0)

    def finish(slot):
        found = jnp.max(col_acc[slot], 0, keepdims=True)
        turned = jnp.max(row_acc[slot].T, 0, keepdims=True)
        result[pl.ds(slot, 1)] = jnp.maximum(found, turned)

    @pl.when(inner)
    def _():
        at_right = x == 1
        relays = jnp.logical_and(leads, at_right)
        forwards = jnp.logical_and(leads, x == 0)
        cross = jnp.where(low, 0, 1)
        for slot in range(SLOTS):
            if slot < 4:
                shard = line_z(slot) * 4 + x * 2 + c
            elif slot < 6:
                shard = line_z(slot - 4) * 4 + x * 2 + 1 - c
            else:
                shard = line_z(slot - 6) * 4 + cross
            flat = jnp.where(places[shard] >= 0, 0.0, FLOOR)
            col_bias[slot] = flat
            tall = jnp.broadcast_to(flat, (LANES, padded)).T
            row_bias[slot] = tall
        pair(0, 0, same=True)
        for k in every:

            @pl.when(relays)
            def _():
                arrived(6, k)
                copy(6, 6, 4, k, sister).start()

            arrived(1, k)
            copy(1, 3, 1, k, peer).start()
            copy(1, 5, 3, k, sister).start()

            @pl.when(forwards)
            def _():
                copy(1, 7, 5, k, across).start()

        for k in every:
            arrived(2, k)

            @pl.when(forwards)
            def _():
                copy(2, 8, 6, k, across).start()

        for k in every:
            arrived(4, k)
            arrived(5, k)
        pair(1, 0)
        pair(1, 1, same=True)

        @pl.when(jnp.logical_not(leads))
        def _():
            each(0, 4, lambda i: pair(i // 2, 4 + i % 2))

        first = jnp.where(leads, 0, 2)

        def against(slot):
            each(first, 4, lambda i: pair(slot, i + 2 * (i // 2)))

        against(2)

        @pl.when(forwards)
        def _():
            for k in every:
                arrived(3, k)
                copy(3, 9, 7, k, across).start()

        @pl.when(at_right)
        def _():
            for j in range(3):
                for k in every:
                    if j == 0:

                        @pl.when(jnp.logical_not(leads))
                        def _():
                            arrived(6, k)

                    else:
                        arrived(6 + j, k)

                        @pl.when(leads)
                        def _():
                            copy(6 + j, 6 + j, 4 + j, k, sister).start()

                each(0, 3, lambda i: pair(6 + j, i))

        @pl.when(jnp.logical_not(forwards))
        def _():
            for k in every:
                arrived(3, k)

        against(3)

        @pl.when(at_right)
        def _():
            each(6, 9, lambda i: pair(i, 3))
            for k in every:
                arrived(9, k)

                @pl.when(leads)
                def _():
                    copy(9, 9, 7, k, sister).start()

            each(0, 4, lambda i: pair(9, i))

        for slot in range(SLOTS):
            finish(slot)
        gathered[rank] = result[...]

    def final_copy(step, target, origin):
        return pltpu.make_async_remote_copy(
            src_ref=result,
            dst_ref=gathered.at[origin],
            send_sem=final_send.at[step],
            recv_sem=final_recv.at[origin],
            device_id=where_is(target),
            device_id_type=pl.DeviceIdType.MESH,
        )

    @pl.when(inner)
    def _():
        for step in range(1, 16):
            final_copy(step, (me + step) % 16, rank).start()

    for origin in range(8):

        @pl.when(me != 4 + origin)
        def _():
            final_copy(1, (me + 1) % 16, origin).wait_recv()

    mine = lax.broadcasted_iota(jnp.int32, (OWN, LANES), 0) + me * OWN
    best = jnp.full((OWN, LANES), FLOOR, jnp.float32)
    for shard in range(16):
        sz, sx, sc = shard // 4, (shard // 2) % 2, shard % 2
        value = None

        def add(value, origin, slot):
            got = gathered[origin, slot : slot + 1]
            return got if value is None else jnp.maximum(value, got)

        for level in (1, 2):
            line = (1, 0, 2, 3) if level == 1 else (2, 3, 1, 0)
            turn = line.index(sz)
            value = add(value, (level - 1) * 4 + sx * 2 + sc, turn)
            if turn < 2:
                value = add(value, (level - 1) * 4 + sx * 2 + 1 - sc, 4 + turn)
            if sx == 0 and sc == level - 1:
                for core in (0, 1):
                    value = add(value, (level - 1) * 4 + 2 + core, 6 + turn)
        place = places[shard]
        for j in range(padded // LANES):
            lanes = slice(j * LANES, (j + 1) * LANES)
            best = jnp.maximum(best, jnp.where(place[:, lanes] == mine, value[:, lanes], FLOOR))
    final_acc[:OWN] = best
    final_acc[OWN:] = jnp.full((final_acc.shape[0] - OWN, LANES), FLOOR, jnp.float32)
    out_ref[...] = jnp.max(final_acc[...].T, 0, keepdims=True)

    for step in range(1, 16):
        place_copy(step, me, (me + step) % 16).wait_send()

    @pl.when(jnp.logical_not(inner))
    def _():
        for k in every:
            copy(0, 1, 0, k, inward).wait_send()

    @pl.when(inner)
    def _():
        for k in every:
            copy(0, 2, 0, k, peer).wait_send()
            copy(1, 3, 1, k, peer).wait_send()
            copy(0, 4, 2, k, sister).wait_send()
            copy(1, 5, 3, k, sister).wait_send()

            @pl.when(leads)
            def _():
                for turn in range(4):
                    copy(6 + turn, 6 + turn, 4 + turn, k, sister).wait_send()

        for step in range(1, 16):
            final_copy(step, (me + step) % 16, rank).wait_send()


def line_body(shard_rows, row_position, shard_count):
    capacity, feature = shard_rows.shape
    sent = -(-capacity // 16) * 16
    padded = -(-capacity // LANES) * LANES
    pieces = 3
    size = -(-sent // (16 * pieces)) * 16
    chunks = [(begin, min(size, sent - begin)) for begin in range(0, sent, size)]
    slot_index = jnp.arange(padded)
    place = jnp.where(
        slot_index < shard_count[0], jnp.pad(row_position, (0, padded - capacity)), -1
    )[None, :]
    tall = -(-OWN // LANES) * LANES
    found = pl.pallas_call(
        functools.partial(line_kernel, capacity, sent, padded, chunks),
        out_shape=jax.ShapeDtypeStruct((1, tall), jnp.float32),
        in_specs=[pl.BlockSpec(memory_space=pltpu.VMEM)] * 2,
        out_specs=pl.BlockSpec(memory_space=pltpu.VMEM),
        scratch_shapes=[
            pltpu.VMEM((SLOTS, padded, feature), jnp.bfloat16),
            pltpu.VMEM((16, 1, padded), jnp.int32),
            pltpu.VMEM((SLOTS, padded, LANES), jnp.float32),
            pltpu.VMEM((SLOTS, 8, padded), jnp.float32),
            pltpu.VMEM((SLOTS, padded, LANES), jnp.float32),
            pltpu.VMEM((SLOTS, 1, padded), jnp.float32),
            pltpu.VMEM((16, padded), jnp.float32),
            pltpu.VMEM((8, 16, padded), jnp.float32),
            pltpu.VMEM((tall, LANES), jnp.float32),
            pltpu.SemaphoreType.DMA((8, len(chunks))),
            pltpu.SemaphoreType.DMA((SLOTS, len(chunks))),
            pltpu.SemaphoreType.DMA((16,)),
            pltpu.SemaphoreType.DMA((16,)),
            pltpu.SemaphoreType.DMA((16,)),
            pltpu.SemaphoreType.DMA((8,)),
        ],
        compiler_params=pltpu.CompilerParams(collective_id=0, has_side_effects=True),
    )(shard_rows, place)
    return found[0, :OWN]


def solution(mesh):
    sizes = tuple(mesh.shape[axis] for axis in ("row", "col", "rep"))
    return jax.shard_map(
        line_body if sizes == (4, 2, 2) else body,
        mesh=mesh,
        in_specs=(
            P(("grp", "row", "col", "rep"), None),
            P(("grp", "row", "col", "rep")),
            P(("grp", "row", "col", "rep")),
        ),
        out_specs=P(("grp", "row", "col", "rep")),
        check_vma=False,
    )
```

```python
import functools
import math

import jax
import jax.numpy as jnp
from jax import lax
from jax.experimental import pallas as pl
from jax.experimental.pallas import tpu as pltpu
from jax.sharding import PartitionSpec as P

OWN = 192


def normalize(owned_rows):
    widened = owned_rows.astype(jnp.float32)
    return (widened / jnp.sqrt(jnp.sum(widened * widened, 1, keepdims=True) + 1e-06)).astype(
        jnp.bfloat16
    )


def body(shard_rows, row_position, shard_count):
    row_devices = lax.axis_size("row")
    cross_devices = lax.axis_size(("col", "rep"))
    all_shards = row_devices * cross_devices
    per_owner = OWN
    owner_load = max(1, per_owner // all_shards)
    slot_count = 2 * owner_load
    block_rows = per_owner * cross_devices
    capacity, feature = shard_rows.shape
    row_place = lax.axis_index("row")
    cross_place = lax.axis_index(("col", "rep"))
    is_used = jnp.arange(capacity) < shard_count[0]
    position = jnp.where(is_used, row_position, 0)
    owner_first = position // per_owner
    one_hot = jnp.logical_and(
        owner_first[:, None] == jnp.arange(all_shards)[None, :], is_used[:, None]
    ).astype(jnp.int32)
    ranking = jnp.sum(jnp.cumsum(one_hot, 0) * one_hot, 1) - 1
    target = jnp.where(is_used, owner_first * slot_count + ranking, all_shards * slot_count)
    packed = (
        jnp.zeros((all_shards * slot_count, feature), shard_rows.dtype)
        .at[target]
        .set(shard_rows, mode="drop")
    )
    placed = (
        jnp.full((all_shards * slot_count,), -1, jnp.int32).at[target].set(position, mode="drop")
    )
    first_packed = packed.reshape(row_devices, cross_devices, slot_count, feature)
    first_placed = placed.reshape(row_devices, cross_devices, slot_count)
    own_offset = row_place * block_rows + cross_place * per_owner
    received = (
        lax.all_to_all(
            lax.all_to_all(first_packed, "row", split_axis=0, concat_axis=0, tiled=True),
            ("col", "rep"),
            split_axis=1,
            concat_axis=1,
            tiled=True,
        ),
        lax.all_to_all(
            lax.all_to_all(first_placed, "row", split_axis=0, concat_axis=0, tiled=True),
            ("col", "rep"),
            split_axis=1,
            concat_axis=1,
            tiled=True,
        ),
    )
    flat_rows = received[0].reshape(-1, feature)
    flat_places = received[1].reshape(-1)
    local_index = jnp.where(flat_places >= 0, flat_places - own_offset, per_owner)
    owned_rows = (
        jnp.zeros((per_owner, feature), flat_rows.dtype).at[local_index].set(flat_rows, mode="drop")
    )
    row_owned = normalize(owned_rows)
    row_block = lax.all_gather(row_owned, ("col", "rep"), axis=0, tiled=True)
    column_index = jnp.arange(block_rows)
    column_block = lax.all_gather(row_owned, "row", axis=0, tiled=True)
    column_places = (
        column_index // per_owner * block_rows + cross_place * per_owner + column_index % per_owner
    )
    row_step = math.gcd(block_rows, 512)
    column_step = math.gcd(block_rows, 1024)

    def row_maxima(inputs):
        row_tile, row_start = inputs
        row_global = row_place * block_rows + row_start + jnp.arange(row_step)
        running = jnp.full((row_step,), -4.0, jnp.float32)
        for column_turn in range(block_rows // column_step):
            column_tile = column_block[column_turn * column_step : (column_turn + 1) * column_step]
            scores = jnp.einsum(
                "rd,cd->rc", row_tile, column_tile, preferred_element_type=jnp.float32
            )
            column_global = column_places[
                column_turn * column_step : (column_turn + 1) * column_step
            ]
            scores = jnp.where(row_global[:, None] == column_global[None, :], -4.0, scores)
            running = jnp.maximum(running, jnp.max(scores, 1))
        return running

    starts = jnp.arange(block_rows // row_step, dtype=jnp.int32) * row_step
    maxima = lax.map(row_maxima, (row_block.reshape(-1, row_step, feature), starts)).reshape(
        block_rows
    )
    combined = lax.pmax(maxima, ("col", "rep"))
    return lax.dynamic_slice_in_dim(combined, cross_place * per_owner, per_owner)


FLOOR = -8.0
LANES = 128
SLOTS = 10


def line_kernel(
    capacity, sent, padded, chunks,
    rows_ref, place_ref, out_ref,
    buf, slot_place, places, row_acc, col_acc, row_bias, col_bias, result, gathered, final_acc,
    send_sem, recv_sem, place_send, place_recv, final_send, final_recv,
):
    z, x, c = lax.axis_index("row"), lax.axis_index("col"), lax.axis_index("rep")
    me = z * 4 + x * 2 + c
    inner = jnp.logical_and(z >= 1, z <= 2)
    low = z <= 1
    leads = c == z - 1
    rank = (z - 1) * 4 + x * 2 + c

    def where_is(device):
        return {"row": device // 4, "col": (device // 2) % 2, "rep": device % 2}

    def at(zz, xx, cc):
        return {"row": zz, "col": xx, "rep": cc}

    sister = at(z, x, 1 - c)
    across = at(z, 1 - x, c)
    greeted = [sister, across, at(z, 1 - x, 1 - c)]
    barrier = pltpu.get_barrier_semaphore()

    def greet(device):
        pl.semaphore_signal(
            barrier, inc=1, device_id=device, device_id_type=pl.DeviceIdType.MESH
        )

    for device in greeted:
        greet(device)

    @pl.when(z >= 1)
    def _():
        greet(at(z - 1, x, c))

    @pl.when(z <= 2)
    def _():
        greet(at(z + 1, x, c))

    widened = rows_ref[...].astype(jnp.float32)
    scale = jnp.sqrt(jnp.sum(widened * widened, 1, keepdims=True) + 1e-06)
    buf[0, :capacity] = (widened / scale).astype(jnp.bfloat16)
    if padded > capacity:
        buf[0, capacity:] = jnp.zeros((padded - capacity, buf.shape[2]), jnp.bfloat16)
    slot_place[0] = place_ref[...]

    @pl.when(inner)
    def _():
        if padded > sent:
            for slot in range(1, SLOTS):
                buf[slot, sent:] = jnp.zeros((padded - sent, buf.shape[2]), jnp.bfloat16)
        row_acc[...] = jnp.full(row_acc.shape, FLOOR, jnp.float32)
        col_acc[...] = jnp.full(col_acc.shape, FLOOR, jnp.float32)
        result[...] = jnp.full(result.shape, FLOOR, jnp.float32)

    @pl.when(inner)
    def _():
        pl.semaphore_wait(barrier, 5)

    @pl.when(jnp.logical_not(inner))
    def _():
        pl.semaphore_wait(barrier, 4)

    def copy(src, dst, kind, k, device):
        if k == len(chunks):
            src_ref = place_ref if src == 0 else slot_place.at[src]
            dst_ref = slot_place.at[dst]
        else:
            begin, count = chunks[k]
            src_ref = buf.at[src, pl.ds(begin, count)]
            dst_ref = buf.at[dst, pl.ds(begin, count)]
        return pltpu.make_async_remote_copy(
            src_ref=src_ref,
            dst_ref=dst_ref,
            send_sem=send_sem.at[kind, k],
            recv_sem=recv_sem.at[dst, k],
            device_id=device,
            device_id_type=pl.DeviceIdType.MESH,
        )

    every = [len(chunks)] + list(range(len(chunks)))
    inward = at(jnp.where(low, 1, 2), x, c)
    peer = at(3 - z, x, c)

    def arrived(slot, k):
        copy(1, slot, 0, k, sister).wait_recv()

    @pl.when(jnp.logical_not(inner))
    def _():
        for k in every:
            copy(0, 1, 0, k, inward).start()

    @pl.when(inner)
    def _():
        for k in every:
            copy(0, 2, 0, k, peer).start()
            copy(0, 6, 4, k, across).start()
            copy(0, 4, 2, k, sister).start()

    def place_copy(step, target, origin):
        return pltpu.make_async_remote_copy(
            src_ref=slot_place.at[pl.ds(0, 2)],
            dst_ref=places.at[origin],
            send_sem=place_send.at[step],
            recv_sem=place_recv.at[origin],
            device_id=where_is(target),
            device_id_type=pl.DeviceIdType.MESH,
        )

    def pair(a, b, same=False):
        scores = lax.dot_general(
            buf[a], buf[b], (((1,), (1,)), ((), ())), preferred_element_type=jnp.float32
        )
        if same:
            row_id = lax.broadcasted_iota(jnp.int32, scores.shape, 0)
            col_id = lax.broadcasted_iota(jnp.int32, scores.shape, 1)
            scores = jnp.where(row_id == col_id, FLOOR, scores)
        bias = row_bias[a]
        running = None if same else row_acc[a]
        for j in range(padded // LANES):
            lanes = slice(j * LANES, (j + 1) * LANES)
            part = scores[:, lanes]
            down = jnp.max((part + bias).reshape(padded // 8, 8, LANES), 0)
            col_acc[b, :, lanes] = jnp.maximum(col_acc[b, :, lanes], down)
            if not same:
                running = jnp.maximum(running, part + col_bias[b][:, lanes])
        if not same:
            row_acc[a] = running

    def each(begin, end, fn):
        def step(i, carry):
            fn(i)
            return carry

        lax.fori_loop(begin, end, step, 0)

    def finish(slot):
        found = jnp.max(col_acc[slot], 0, keepdims=True)
        if slot < 4:
            found = jnp.maximum(found, jnp.max(row_acc[slot].T, 0, keepdims=True))
        result[slot] = found

    @pl.when(inner)
    def _():
        def set_bias(slot):
            flat = jnp.where(slot_place[slot] >= 0, 0.0, FLOOR)
            col_bias[slot] = flat
            row_bias[slot] = jnp.broadcast_to(flat, (LANES, padded)).T

        set_bias(0)
        pair(0, 0, same=True)
        for k in every:
            arrived(6, k)
            copy(6, 8, 6, k, sister).start()
            arrived(1, k)
            copy(1, 3, 1, k, peer).start()
            copy(1, 7, 5, k, across).start()
            copy(1, 5, 3, k, sister).start()
        for slot in (2, 4, 5, 8):
            for k in every:
                arrived(slot, k)
        for slot in (1, 2, 4, 5, 6, 8):
            set_bias(slot)
        pair(1, 0)
        pair(1, 1, same=True)

        @pl.when(jnp.logical_not(leads))
        def _():
            each(0, 4, lambda i: pair(i // 2, 4 + i % 2))

        first = jnp.where(leads, 0, 2)
        across_turn = 2 * x

        def against(slot):
            each(first, 4, lambda i: pair(slot, i + 2 * (i // 2)))

        against(2)
        arrived(3, len(chunks))
        places[rank] = slot_place[:2]
        for step in range(1, 16):
            place_copy(step, (me + step) % 16, rank).start()
        each(0, 2, lambda i: pair(across_turn, 6 + 2 * i))

        @pl.when(x == 0)
        def _():
            each(0, 2, lambda i: pair(1, 6 + 2 * i))

        for k in every:
            arrived(7, k)
            copy(7, 9, 7, k, sister).start()
        set_bias(7)
        pair(across_turn, 7)
        for k in every[1:]:
            arrived(3, k)
        set_bias(3)
        against(3)

        @pl.when(x == 1)
        def _():
            each(0, 2, lambda i: pair(3, 6 + 2 * i))

        pair(across_turn + 1, 7)
        for k in every:
            arrived(9, k)
        set_bias(9)
        each(0, 2, lambda i: pair(across_turn + i, 9))
        for slot in range(SLOTS):
            finish(slot)
        gathered[rank] = result[...]

    def final_copy(step, target, origin):
        return pltpu.make_async_remote_copy(
            src_ref=result,
            dst_ref=gathered.at[origin],
            send_sem=final_send.at[step],
            recv_sem=final_recv.at[origin],
            device_id=where_is(target),
            device_id_type=pl.DeviceIdType.MESH,
        )

    @pl.when(inner)
    def _():
        for step in range(1, 16):
            final_copy(step, (me + step) % 16, rank).start()

    for origin in range(8):

        @pl.when(me != 4 + origin)
        def _():
            place_copy(1, (me + 1) % 16, origin).wait_recv()
            final_copy(1, (me + 1) % 16, origin).wait_recv()

    mine = lax.broadcasted_iota(jnp.int32, (OWN, LANES), 0) + me * OWN
    best = jnp.full((OWN, LANES), FLOOR, jnp.float32)
    for shard in range(16):
        sz, sx, sc = shard // 4, (shard // 2) % 2, shard % 2
        value = None

        def add(value, origin, slot):
            got = gathered[origin, slot]
            return got if value is None else jnp.maximum(value, got)

        for level in (1, 2):
            line = (1, 0, 2, 3) if level == 1 else (2, 3, 1, 0)
            turn = line.index(sz)
            value = add(value, (level - 1) * 4 + sx * 2 + sc, turn)
            if turn < 2:
                value = add(value, (level - 1) * 4 + sx * 2 + 1 - sc, 4 + turn)
                for core in (0, 1):
                    origin = (level - 1) * 4 + (1 - sx) * 2 + core
                    value = add(value, origin, 6 + turn + 2 * (core ^ sc))
        level = 1 if sz <= 1 else 2
        turn = ((1, 0) if level == 1 else (2, 3)).index(sz)
        place = places[(level - 1) * 4 + sx * 2 + sc, turn]
        for j in range(padded // LANES):
            lanes = slice(j * LANES, (j + 1) * LANES)
            best = jnp.maximum(best, jnp.where(place[:, lanes] == mine, value[:, lanes], FLOOR))
    final_acc[:OWN] = best
    final_acc[OWN:] = jnp.full((final_acc.shape[0] - OWN, LANES), FLOOR, jnp.float32)
    out_ref[...] = jnp.max(final_acc[...].T, 0, keepdims=True)

    @pl.when(jnp.logical_not(inner))
    def _():
        for k in every:
            copy(0, 1, 0, k, inward).wait_send()

    @pl.when(inner)
    def _():
        for k in every:
            copy(0, 2, 0, k, peer).wait_send()
            copy(1, 3, 1, k, peer).wait_send()
            copy(0, 4, 2, k, sister).wait_send()
            copy(1, 5, 3, k, sister).wait_send()

            copy(0, 6, 4, k, across).wait_send()
            copy(1, 7, 5, k, across).wait_send()
            copy(6, 8, 6, k, sister).wait_send()
            copy(7, 9, 7, k, sister).wait_send()

        for step in range(1, 16):
            place_copy(step, (me + step) % 16, rank).wait_send()
            final_copy(step, (me + step) % 16, rank).wait_send()


def line_body(shard_rows, row_position, shard_count):
    capacity, feature = shard_rows.shape
    sent = -(-capacity // 16) * 16
    padded = -(-capacity // LANES) * LANES
    pieces = 3
    size = -(-sent // (16 * pieces)) * 16
    chunks = [(begin, min(size, sent - begin)) for begin in range(0, sent, size)]
    slot_index = jnp.arange(padded)
    place = jnp.where(
        slot_index < shard_count[0], jnp.pad(row_position, (0, padded - capacity)), -1
    )[None, :]
    tall = -(-OWN // LANES) * LANES
    found = pl.pallas_call(
        functools.partial(line_kernel, capacity, sent, padded, chunks),
        out_shape=jax.ShapeDtypeStruct((1, tall), jnp.float32),
        in_specs=[pl.BlockSpec(memory_space=pltpu.VMEM)] * 2,
        out_specs=pl.BlockSpec(memory_space=pltpu.VMEM),
        scratch_shapes=[
            pltpu.VMEM((SLOTS, padded, feature), jnp.bfloat16),
            pltpu.VMEM((SLOTS, 1, padded), jnp.int32),
            pltpu.VMEM((8, 2, 1, padded), jnp.int32),
            pltpu.VMEM((4, padded, LANES), jnp.float32),
            pltpu.VMEM((SLOTS, 8, padded), jnp.float32),
            pltpu.VMEM((SLOTS, padded, LANES), jnp.float32),
            pltpu.VMEM((SLOTS, 1, padded), jnp.float32),
            pltpu.VMEM((SLOTS, 1, padded), jnp.float32),
            pltpu.VMEM((8, SLOTS, 1, padded), jnp.float32),
            pltpu.VMEM((tall, LANES), jnp.float32),
            pltpu.SemaphoreType.DMA((8, len(chunks) + 1)),
            pltpu.SemaphoreType.DMA((SLOTS, len(chunks) + 1)),
            pltpu.SemaphoreType.DMA((16,)),
            pltpu.SemaphoreType.DMA((8,)),
            pltpu.SemaphoreType.DMA((16,)),
            pltpu.SemaphoreType.DMA((8,)),
        ],
        compiler_params=pltpu.CompilerParams(collective_id=0, has_side_effects=True),
    )(shard_rows, place)
    return found[0, :OWN]


def solution(mesh):
    sizes = tuple(mesh.shape[axis] for axis in ("row", "col", "rep"))
    return jax.shard_map(
        line_body if sizes == (4, 2, 2) else body,
        mesh=mesh,
        in_specs=(
            P(("grp", "row", "col", "rep"), None),
            P(("grp", "row", "col", "rep")),
            P(("grp", "row", "col", "rep")),
        ),
        out_specs=P(("grp", "row", "col", "rep")),
        check_vma=False,
    )
```

```python
import functools
import math

import jax
import jax.numpy as jnp
from jax import lax
from jax.experimental import pallas as pl
from jax.experimental.pallas import tpu as pltpu
from jax.sharding import PartitionSpec as P

OWN = 192


def normalize(owned_rows):
    widened = owned_rows.astype(jnp.float32)
    return (widened / jnp.sqrt(jnp.sum(widened * widened, 1, keepdims=True) + 1e-06)).astype(
        jnp.bfloat16
    )


def body(shard_rows, row_position, shard_count):
    row_devices = lax.axis_size("row")
    cross_devices = lax.axis_size(("col", "rep"))
    all_shards = row_devices * cross_devices
    per_owner = OWN
    owner_load = max(1, per_owner // all_shards)
    slot_count = 2 * owner_load
    block_rows = per_owner * cross_devices
    capacity, feature = shard_rows.shape
    row_place = lax.axis_index("row")
    cross_place = lax.axis_index(("col", "rep"))
    is_used = jnp.arange(capacity) < shard_count[0]
    position = jnp.where(is_used, row_position, 0)
    owner_first = position // per_owner
    one_hot = jnp.logical_and(
        owner_first[:, None] == jnp.arange(all_shards)[None, :], is_used[:, None]
    ).astype(jnp.int32)
    ranking = jnp.sum(jnp.cumsum(one_hot, 0) * one_hot, 1) - 1
    target = jnp.where(is_used, owner_first * slot_count + ranking, all_shards * slot_count)
    packed = (
        jnp.zeros((all_shards * slot_count, feature), shard_rows.dtype)
        .at[target]
        .set(shard_rows, mode="drop")
    )
    placed = (
        jnp.full((all_shards * slot_count,), -1, jnp.int32).at[target].set(position, mode="drop")
    )
    first_packed = packed.reshape(row_devices, cross_devices, slot_count, feature)
    first_placed = placed.reshape(row_devices, cross_devices, slot_count)
    own_offset = row_place * block_rows + cross_place * per_owner
    received = (
        lax.all_to_all(
            lax.all_to_all(first_packed, "row", split_axis=0, concat_axis=0, tiled=True),
            ("col", "rep"),
            split_axis=1,
            concat_axis=1,
            tiled=True,
        ),
        lax.all_to_all(
            lax.all_to_all(first_placed, "row", split_axis=0, concat_axis=0, tiled=True),
            ("col", "rep"),
            split_axis=1,
            concat_axis=1,
            tiled=True,
        ),
    )
    flat_rows = received[0].reshape(-1, feature)
    flat_places = received[1].reshape(-1)
    local_index = jnp.where(flat_places >= 0, flat_places - own_offset, per_owner)
    owned_rows = (
        jnp.zeros((per_owner, feature), flat_rows.dtype).at[local_index].set(flat_rows, mode="drop")
    )
    row_owned = normalize(owned_rows)
    row_block = lax.all_gather(row_owned, ("col", "rep"), axis=0, tiled=True)
    column_index = jnp.arange(block_rows)
    column_block = lax.all_gather(row_owned, "row", axis=0, tiled=True)
    column_places = (
        column_index // per_owner * block_rows + cross_place * per_owner + column_index % per_owner
    )
    row_step = math.gcd(block_rows, 512)
    column_step = math.gcd(block_rows, 1024)

    def row_maxima(inputs):
        row_tile, row_start = inputs
        row_global = row_place * block_rows + row_start + jnp.arange(row_step)
        running = jnp.full((row_step,), -4.0, jnp.float32)
        for column_turn in range(block_rows // column_step):
            column_tile = column_block[column_turn * column_step : (column_turn + 1) * column_step]
            scores = jnp.einsum(
                "rd,cd->rc", row_tile, column_tile, preferred_element_type=jnp.float32
            )
            column_global = column_places[
                column_turn * column_step : (column_turn + 1) * column_step
            ]
            scores = jnp.where(row_global[:, None] == column_global[None, :], -4.0, scores)
            running = jnp.maximum(running, jnp.max(scores, 1))
        return running

    starts = jnp.arange(block_rows // row_step, dtype=jnp.int32) * row_step
    maxima = lax.map(row_maxima, (row_block.reshape(-1, row_step, feature), starts)).reshape(
        block_rows
    )
    combined = lax.pmax(maxima, ("col", "rep"))
    return lax.dynamic_slice_in_dim(combined, cross_place * per_owner, per_owner)


FLOOR = -8.0
LANES = 128
SLOTS = 10


def line_kernel(
    capacity, sent, padded, chunks,
    rows_ref, raw_ref, count_ref, out_ref,
    buf, slot_place, places, row_acc, col_acc, row_bias, col_bias, result, gathered, final_acc,
    send_sem, recv_sem, place_send, place_recv, final_send, final_recv,
):
    z, x, c = lax.axis_index("row"), lax.axis_index("col"), lax.axis_index("rep")
    me = z * 4 + x * 2 + c
    inner = jnp.logical_and(z >= 1, z <= 2)
    low = z <= 1
    leads = c == z - 1
    rank = (z - 1) * 4 + x * 2 + c

    def where_is(device):
        return {"row": device // 4, "col": (device // 2) % 2, "rep": device % 2}

    def at(zz, xx, cc):
        return {"row": zz, "col": xx, "rep": cc}

    sister = at(z, x, 1 - c)
    across = at(z, 1 - x, c)
    greeted = [sister, across, at(z, 1 - x, 1 - c)]
    barrier = pltpu.get_barrier_semaphore()

    def greet(device):
        pl.semaphore_signal(
            barrier, inc=1, device_id=device, device_id_type=pl.DeviceIdType.MESH
        )

    for device in greeted:
        greet(device)

    @pl.when(z >= 1)
    def _():
        greet(at(z - 1, x, c))

    @pl.when(z <= 2)
    def _():
        greet(at(z + 1, x, c))

    widened = rows_ref[...].astype(jnp.float32)
    scale = jnp.sqrt(jnp.sum(widened * widened, 1, keepdims=True) + 1e-06)
    buf[0, :capacity] = (widened / scale).astype(jnp.bfloat16)
    if padded > capacity:
        buf[0, capacity:] = jnp.zeros((padded - capacity, buf.shape[2]), jnp.bfloat16)
    slot_place[0] = jnp.full((1, padded), -1, jnp.int32)
    slot_place[0, 0, pl.ds(0, capacity)] = raw_ref[...]
    slot_id = lax.broadcasted_iota(jnp.int32, (1, padded), 1)
    slot_place[0] = jnp.where(slot_id < count_ref[0], slot_place[0], -1)

    @pl.when(inner)
    def _():
        if padded > sent:
            for slot in range(1, SLOTS):
                buf[slot, sent:] = jnp.zeros((padded - sent, buf.shape[2]), jnp.bfloat16)
        row_acc[...] = jnp.full(row_acc.shape, FLOOR, jnp.float32)
        col_acc[...] = jnp.full(col_acc.shape, FLOOR, jnp.float32)
        result[...] = jnp.full(result.shape, FLOOR, jnp.float32)

    @pl.when(inner)
    def _():
        pl.semaphore_wait(barrier, 5)

    @pl.when(jnp.logical_not(inner))
    def _():
        pl.semaphore_wait(barrier, 4)

    def copy(src, dst, kind, k, device):
        if k == len(chunks):
            src_ref = slot_place.at[src]
            dst_ref = slot_place.at[dst]
        else:
            begin, count = chunks[k]
            src_ref = buf.at[src, pl.ds(begin, count)]
            dst_ref = buf.at[dst, pl.ds(begin, count)]
        return pltpu.make_async_remote_copy(
            src_ref=src_ref,
            dst_ref=dst_ref,
            send_sem=send_sem.at[kind, k],
            recv_sem=recv_sem.at[dst, k],
            device_id=device,
            device_id_type=pl.DeviceIdType.MESH,
        )

    every = [len(chunks)] + list(range(len(chunks)))
    inward = at(jnp.where(low, 1, 2), x, c)
    peer = at(3 - z, x, c)

    def arrived(slot, k):
        copy(1, slot, 0, k, sister).wait_recv()

    @pl.when(jnp.logical_not(inner))
    def _():
        for k in every:
            copy(0, 1, 0, k, inward).start()

    @pl.when(inner)
    def _():
        for k in every:
            copy(0, 2, 0, k, peer).start()
            copy(0, 6, 4, k, across).start()
            copy(0, 4, 2, k, sister).start()

    def place_copy(step, target, origin):
        return pltpu.make_async_remote_copy(
            src_ref=slot_place.at[pl.ds(0, 2)],
            dst_ref=places.at[origin],
            send_sem=place_send.at[step],
            recv_sem=place_recv.at[origin],
            device_id=where_is(target),
            device_id_type=pl.DeviceIdType.MESH,
        )

    def pair(a, b, same=False):
        scores = lax.dot_general(
            buf[a], buf[b], (((1,), (1,)), ((), ())), preferred_element_type=jnp.float32
        )
        if same:
            row_id = lax.broadcasted_iota(jnp.int32, scores.shape, 0)
            col_id = lax.broadcasted_iota(jnp.int32, scores.shape, 1)
            scores = jnp.where(row_id == col_id, FLOOR, scores)
        bias = row_bias[a]
        running = None if same else row_acc[a]
        for j in range(padded // LANES):
            lanes = slice(j * LANES, (j + 1) * LANES)
            part = scores[:, lanes]
            down = jnp.max((part + bias).reshape(padded // 8, 8, LANES), 0)
            col_acc[b, :, lanes] = jnp.maximum(col_acc[b, :, lanes], down)
            if not same:
                running = jnp.maximum(running, part + col_bias[b][:, lanes])
        if not same:
            row_acc[a] = running

    def double(a, b):
        rows = buf[pl.ds(a, 2)].reshape(2 * padded, buf.shape[2])
        scores = lax.dot_general(
            rows, buf[b], (((1,), (1,)), ((), ())), preferred_element_type=jnp.float32
        )
        for half in range(2):
            bias = row_bias[a + half]
            running = row_acc[a + half]
            for j in range(padded // LANES):
                lanes = slice(j * LANES, (j + 1) * LANES)
                part = scores[half * padded : (half + 1) * padded, lanes]
                down = jnp.max((part + bias).reshape(padded // 8, 8, LANES), 0)
                col_acc[b, :, lanes] = jnp.maximum(col_acc[b, :, lanes], down)
                running = jnp.maximum(running, part + col_bias[b][:, lanes])
            row_acc[a + half] = running

    def each(begin, end, fn):
        def step(i, carry):
            fn(i)
            return carry

        lax.fori_loop(begin, end, step, 0)

    def finish(slot):
        found = jnp.max(col_acc[slot], 0, keepdims=True)
        if slot < 8:
            found = jnp.maximum(found, jnp.max(row_acc[slot].T, 0, keepdims=True))
        result[slot] = found

    @pl.when(inner)
    def _():
        def set_bias(slot):
            flat = jnp.where(slot_place[slot] >= 0, 0.0, FLOOR)
            col_bias[slot] = flat
            row_bias[slot] = jnp.broadcast_to(flat, (LANES, padded)).T

        set_bias(0)
        pair(0, 0, same=True)
        for k in every:
            arrived(1, k)
            copy(1, 3, 1, k, peer).start()
            copy(1, 8, 5, k, across).start()
            copy(1, 5, 3, k, sister).start()
            arrived(6, k)
            copy(6, 7, 6, k, sister).start()
        for slot in (2, 4, 5, 7):
            for k in every:
                arrived(slot, k)
        for slot in (1, 2, 4, 5, 6, 7):
            set_bias(slot)
        pair(1, 0)
        pair(1, 1, same=True)

        @pl.when(jnp.logical_not(leads))
        def _():
            each(0, 2, lambda i: double(4, i))

        first = jnp.where(leads, 0, 1)
        across_turn = 2 * x

        def against(slot):
            each(first, 2, lambda i: double(4 * i, slot))

        against(2)
        arrived(3, len(chunks))
        places[rank] = slot_place[:2]
        for step in range(1, 16):
            place_copy(step, (me + step) % 16, rank).start()
        each(0, 2 - x, lambda i: double(6, across_turn + i))
        for k in every:
            arrived(8, k)
            copy(8, 9, 7, k, sister).start()
        set_bias(8)

        @pl.when(x == 0)
        def _():
            double(0, 8)

        for k in every[1:]:
            arrived(3, k)
        set_bias(3)
        against(3)

        @pl.when(x == 1)
        def _():
            double(6, 3)

        for k in every:
            arrived(9, k)
        set_bias(9)
        each(jnp.where(x == 0, 9, 8), 10, lambda i: double(across_turn, i))

        for slot in range(SLOTS):
            finish(slot)
        gathered[rank] = result[...]

    def final_copy(step, target, origin):
        return pltpu.make_async_remote_copy(
            src_ref=result,
            dst_ref=gathered.at[origin],
            send_sem=final_send.at[step],
            recv_sem=final_recv.at[origin],
            device_id=where_is(target),
            device_id_type=pl.DeviceIdType.MESH,
        )

    @pl.when(inner)
    def _():
        for step in range(1, 16):
            final_copy(step, (me + step) % 16, rank).start()

    for origin in range(8):

        @pl.when(me != 4 + origin)
        def _():
            place_copy(1, (me + 1) % 16, origin).wait_recv()
            final_copy(1, (me + 1) % 16, origin).wait_recv()

    mine = lax.broadcasted_iota(jnp.int32, (OWN, LANES), 0) + me * OWN
    best = jnp.full((OWN, LANES), FLOOR, jnp.float32)
    for shard in range(16):
        sz, sx, sc = shard // 4, (shard // 2) % 2, shard % 2
        value = None

        def add(value, origin, slot):
            got = gathered[origin, slot]
            return got if value is None else jnp.maximum(value, got)

        for level in (1, 2):
            line = (1, 0, 2, 3) if level == 1 else (2, 3, 1, 0)
            turn = line.index(sz)
            value = add(value, (level - 1) * 4 + sx * 2 + sc, turn)
            if turn < 2:
                value = add(value, (level - 1) * 4 + sx * 2 + 1 - sc, 4 + turn)
                for core in (0, 1):
                    origin = (level - 1) * 4 + (1 - sx) * 2 + core
                    value = add(value, origin, 6 + 2 * turn + (core ^ sc))
        level = 1 if sz <= 1 else 2
        turn = ((1, 0) if level == 1 else (2, 3)).index(sz)
        place = places[(level - 1) * 4 + sx * 2 + sc, turn]
        for j in range(padded // LANES):
            lanes = slice(j * LANES, (j + 1) * LANES)
            best = jnp.maximum(best, jnp.where(place[:, lanes] == mine, value[:, lanes], FLOOR))
    final_acc[:OWN] = best
    final_acc[OWN:] = jnp.full((final_acc.shape[0] - OWN, LANES), FLOOR, jnp.float32)
    out_ref[...] = jnp.max(final_acc[...].T, 0, keepdims=True)[0, :OWN]

    @pl.when(jnp.logical_not(inner))
    def _():
        for k in every:
            copy(0, 1, 0, k, inward).wait_send()

    @pl.when(inner)
    def _():
        for k in every:
            copy(0, 2, 0, k, peer).wait_send()
            copy(1, 3, 1, k, peer).wait_send()
            copy(0, 4, 2, k, sister).wait_send()
            copy(1, 5, 3, k, sister).wait_send()

            copy(0, 6, 4, k, across).wait_send()
            copy(1, 8, 5, k, across).wait_send()
            copy(6, 7, 6, k, sister).wait_send()
            copy(8, 9, 7, k, sister).wait_send()

        for step in range(1, 16):
            place_copy(step, (me + step) % 16, rank).wait_send()
            final_copy(step, (me + step) % 16, rank).wait_send()


def line_body(shard_rows, row_position, shard_count):
    capacity, feature = shard_rows.shape
    sent = -(-capacity // 16) * 16
    padded = -(-capacity // LANES) * LANES
    pieces = 3
    size = -(-sent // (16 * pieces)) * 16
    chunks = [(begin, min(size, sent - begin)) for begin in range(0, sent, size)]
    tall = -(-OWN // LANES) * LANES
    return pl.pallas_call(
        functools.partial(line_kernel, capacity, sent, padded, chunks),
        out_shape=jax.ShapeDtypeStruct((OWN,), jnp.float32),
        in_specs=[
            pl.BlockSpec(memory_space=pltpu.VMEM),
            pl.BlockSpec(memory_space=pltpu.VMEM),
            pl.BlockSpec(memory_space=pltpu.SMEM),
        ],
        out_specs=pl.BlockSpec(memory_space=pltpu.VMEM),
        scratch_shapes=[
            pltpu.VMEM((SLOTS, padded, feature), jnp.bfloat16),
            pltpu.VMEM((SLOTS, 1, padded), jnp.int32),
            pltpu.VMEM((8, 2, 1, padded), jnp.int32),
            pltpu.VMEM((8, padded, LANES), jnp.float32),
            pltpu.VMEM((SLOTS, 8, padded), jnp.float32),
            pltpu.VMEM((SLOTS, padded, LANES), jnp.float32),
            pltpu.VMEM((SLOTS, 1, padded), jnp.float32),
            pltpu.VMEM((SLOTS, 1, padded), jnp.float32),
            pltpu.VMEM((8, SLOTS, 1, padded), jnp.float32),
            pltpu.VMEM((tall, LANES), jnp.float32),
            pltpu.SemaphoreType.DMA((8, len(chunks) + 1)),
            pltpu.SemaphoreType.DMA((SLOTS, len(chunks) + 1)),
            pltpu.SemaphoreType.DMA((16,)),
            pltpu.SemaphoreType.DMA((8,)),
            pltpu.SemaphoreType.DMA((16,)),
            pltpu.SemaphoreType.DMA((8,)),
        ],
        compiler_params=pltpu.CompilerParams(collective_id=0, has_side_effects=True),
    )(shard_rows, row_position, shard_count)


def solution(mesh):
    sizes = tuple(mesh.shape[axis] for axis in ("row", "col", "rep"))
    return jax.shard_map(
        line_body if sizes == (4, 2, 2) else body,
        mesh=mesh,
        in_specs=(
            P(("grp", "row", "col", "rep"), None),
            P(("grp", "row", "col", "rep")),
            P(("grp", "row", "col", "rep")),
        ),
        out_specs=P(("grp", "row", "col", "rep")),
        check_vma=False,
    )
```
